32 devices in a mesh: dp: 8 (over y, x, core), tensor: 4 (over z).
Axes of the slice: x: 2, y: 2, z: 4, core: 2. Of those that a mesh axis runs over, the one named last changes fastest.
Arguments:
- x_in: float32 [4096, 1024], P(('dp', 'tensor')), may hold values from -6 to 6
- d_out: float32 [4096, 1024], P(('dp', 'tensor')), may hold values from -6 to 6
- seq_lengths: int32 [8, 2], P('dp'), may hold values from 128 to 384, as said below
- w_qkv: bfloat16 [2, 1024, 3, 1024], P(None, 'dp', None, 'tensor'), may hold values from -0.1875 to 0.1875
- b_qv: bfloat16 [2, 2, 1024], P(None, None, ('tensor', 'dp')), may hold values from -3 to 3
- w_o: bfloat16 [2, 1024, 1024], P(None, 'tensor', 'dp'), may hold values from -0.5 to 0.5
- w_1: bfloat16 [2, 1024, 4096], P(None, 'dp', 'tensor'), may hold values from -0.1875 to 0.1875
- b_ffn: bfloat16 [2, 4096], P(None, ('tensor', 'dp')), may hold values from -3 to 3
- w_2: bfloat16 [2, 4096, 1024], P(None, 'tensor', 'dp'), may hold values from -0.09375 to 0.09375
- norm_gains: bfloat16 [2, 2, 1024], P(None, None, 'dp'), may hold values from 0.5 to 1.5
- vec_biases: bfloat16 [2, 4, 1024], P(None, None, 'dp'), may hold values from -3 to 3
Outputs:
- output: float32 [4096, 1024], P(('dp', 'tensor'))
- grad_x: float32 [4096, 1024], P(('dp', 'tensor'))
- grad_w_qkv: float32 [2, 1024, 3, 1024], P(None, 'dp', None, 'tensor')
- grad_b_qv: float32 [2, 2, 1024], P(None, None, ('tensor', 'dp'))
- grad_w_o: float32 [2, 1024, 1024], P(None, 'tensor', 'dp')
- grad_w_1: float32 [2, 1024, 4096], P(None, 'dp', 'tensor')
- grad_b_ffn: float32 [2, 4096], P(None, ('tensor', 'dp'))
- grad_w_2: float32 [2, 4096, 1024], P(None, 'tensor', 'dp')
- grad_norm_gains: float32 [2, 2, 1024], P(None, None, 'dp')
- grad_vec_biases: float32 [2, 4, 1024], P(None, None, 'dp')
The draws below stay inside these ranges and needn't reach their ends.
Inputs may be any that keep to these rules, and one draw needn't show every extreme that they name: `seq_lengths`: each row lists the lengths of the 2 sequences of one group in packing order; they sum to 512. Some group holds a sequence of length exactly 384.
All inputs are finite; a program needn't handle non-finite values.
Results may differ from the reference program's by a relative error of at most 0.02.
Values may be sent and summed in bfloat16 or wider, within the bound.
A program may use at most 128 MiB of HBM per device.

```python
import math
import jax
import jax.numpy as jnp
from jax import lax

D = 1024
HEAD_DIM = 64
FF = 4096
LAYERS = 2
TOK_DEV = 512
MOST = 384
TOKENS = 4096
N_DP = 8


def draw_seq_lengths(key, part):
    first_key = jax.random.fold_in(key, 11)
    pick_key = jax.random.fold_in(key, 12)
    flip_key = jax.random.fold_in(key, 13)
    first_len = jax.random.randint(first_key, (N_DP,), TOK_DEV - MOST, MOST + 1, dtype=jnp.int32)
    chosen = jax.random.randint(pick_key, (), 0, N_DP, dtype=jnp.int32)
    group_ids = jnp.arange(N_DP, dtype=jnp.int32)
    first_len = jnp.where(group_ids == chosen, jnp.int32(MOST), first_len).astype(jnp.int32)
    second_len = (TOK_DEV - first_len).astype(jnp.int32)
    flipped = jax.random.randint(flip_key, (N_DP,), 0, 2, dtype=jnp.int32) == 1
    lead = jnp.where(flipped, second_len, first_len)
    trail = jnp.where(flipped, first_len, second_len)
    return jnp.stack([lead, trail], axis=1).astype(jnp.int32)


def spiked(result, key, source, target, blocks, factor):
    owner, partner = [(jnp.arange(result.shape[dim]) // (result.shape[dim] // blocks)).reshape([-1 if axis == dim else 1 for axis in range(result.ndim)]) for dim in (source, target)]
    chosen = jax.random.permutation(key, blocks)[partner]
    strong = (owner == chosen) | (owner == (partner + blocks // 2) % blocks)
    return jnp.where(strong, factor * result, result)


def block_scale(rng, shape, split, least, high):
    loudness = 1.0
    for axis_at, blocks in split:
        steps = jax.random.uniform(jax.random.fold_in(jax.random.fold_in(rng, 6), axis_at), (blocks,), jnp.float32, least / len(split), high / len(split))
        loudness = loudness * jnp.repeat(jnp.exp(steps), shape[axis_at] // blocks).reshape((-1,) + (1,) * (len(shape) - 1 - axis_at))
    return loudness


def noise(key, shape, spread, most, split=(), held_as=jnp.bfloat16):
    factor_of = block_scale(key, shape, split, -0.22, 0.18) if split else 1.0
    values = jax.random.normal(key, shape, jnp.float32) * spread * factor_of
    return jnp.minimum(jnp.maximum(values, -most), most).astype(held_as)


def bell_draw_with(stream_key, shape, scale, reach, split, heavy, kind=jnp.bfloat16):
    result = scale * jax.random.normal(stream_key, shape, jnp.float32)
    if split:
        result = result * block_scale(stream_key, shape, split, -0.22, 0.18)
    return jnp.clip(spiked(result, jax.random.fold_in(stream_key, 3), *heavy), -reach, reach).astype(kind)


def setup_inputs(seed: int = 0) -> dict:
    key_list = jax.random.split(jax.random.key(seed), 12)
    return {
        "x_in": noise(key_list[0], (TOKENS, D), 1.0, 6.0, ((0, 32),), jnp.float32),
        "d_out": bell_draw_with(key_list[1], (TOKENS, D), 1.0, 6.0, ((0, 32),), (0, 1, 32, 2.75), jnp.float32),
        "seq_lengths": draw_seq_lengths(jax.random.fold_in(key_list[11], 71), 0),
        "w_qkv": noise(key_list[3], (LAYERS, D, 3, D), D ** -0.5, 0.1875, ((1, 8), (3, 4))),
        "b_qv": noise(key_list[4], (LAYERS, 2, D), 0.5, 3.0, ((2, 32),)),
        "w_o": noise(key_list[5], (LAYERS, D, D), (D // 8) ** -0.5, 0.5, ((1, 4), (2, 8))),
        "w_1": noise(key_list[6], (LAYERS, D, FF), D ** -0.5, 0.1875, ((1, 8), (2, 4))),
        "b_ffn": noise(key_list[7], (LAYERS, FF), 0.5, 3.0, ((1, 32),)),
        "w_2": noise(key_list[8], (LAYERS, FF, D), FF ** -0.5, 0.09375, ((1, 4), (2, 8))),
        "norm_gains": jnp.clip(1.0 + 0.1 * jax.random.normal(key_list[9], (LAYERS, 2, D), jnp.float32), 0.5, 1.5).astype(jnp.bfloat16),
        "vec_biases": noise(key_list[10], (LAYERS, 4, D), 0.5, 3.0, ((2, 8),)),
    }


NORM_EPS = 1e-05
GELU_COEFF = 0.7978845608028654
GELU_CUBIC = 0.044715

def layer_norm(inputs, gain_row, bias_row):
    row_mean = lax.optimization_barrier(jnp.mean(inputs, axis=-1, keepdims=True))
    centered = inputs - row_mean
    inv_std = lax.rsqrt(lax.optimization_barrier(jnp.mean(centered * centered, axis=-1, keepdims=True)) + NORM_EPS)
    normed = centered * inv_std
    return (normed * gain_row + bias_row, normed, inv_std)

def norm_back(grad_in, normed, inv_std, gain_row):
    scaled = grad_in * gain_row
    return inv_std * (scaled - lax.optimization_barrier(jnp.mean(scaled, axis=-1, keepdims=True)) - normed * lax.optimization_barrier(jnp.mean(scaled * normed, axis=-1, keepdims=True)))

def gelu_pair(pre_act):
    squared = pre_act * pre_act
    tangent = jnp.tanh(GELU_COEFF * (pre_act + GELU_CUBIC * squared * pre_act))
    gelu_value = 0.5 * pre_act * (1.0 + tangent)
    gelu_slope = 0.5 * (1.0 + tangent) + 0.5 * pre_act * (1.0 - tangent * tangent) * GELU_COEFF * (1.0 + 3.0 * GELU_CUBIC * squared)
    return (gelu_value, gelu_slope)

def segment_ids(lengths, total_rows):
    sequence_ends = jnp.cumsum(lengths.astype(jnp.int32)).astype(jnp.int32)
    positions = jnp.arange(total_rows, dtype=jnp.int32)
    return lax.optimization_barrier(jnp.sum((positions[:, None] >= sequence_ends[None, :]).astype(jnp.int32), axis=1, dtype=jnp.int32))

def group_pass(x_group, grad_group, lengths, params):
    w_qkv, b_qv, w_o, w_1, b_ffn, w_2, norm_gains, vec_biases = params
    group_rows = x_group.shape[0]
    width = x_group.shape[1]
    head_count = width // HEAD_DIM
    score_scale = 1.0 / math.sqrt(HEAD_DIM)
    segments = segment_ids(lengths, group_rows)
    positions = jnp.arange(group_rows, dtype=jnp.int32)
    allowed = (segments[:, None] == segments[None, :]) & (positions[None, :] <= positions[:, None])
    caches = []
    hidden_in = x_group
    for layer_index in range(LAYERS):
        gain_rows = norm_gains[layer_index].astype(jnp.float32)
        bias_rows = vec_biases[layer_index].astype(jnp.float32)
        normed_one, unit_one, inv_one = layer_norm(hidden_in, gain_rows[0], bias_rows[0])
        normed_one = normed_one.astype(jnp.bfloat16)
        qkv_matrix = w_qkv[layer_index].reshape(width, 3 * width)
        projected = jnp.dot(normed_one, qkv_matrix, preferred_element_type=jnp.float32).reshape(group_rows, 3, width)
        qv_bias = b_qv[layer_index].astype(jnp.float32)
        queries = (projected[:, 0] + qv_bias[0]).astype(jnp.bfloat16).reshape(group_rows, head_count, HEAD_DIM)
        key_vecs = projected[:, 1].astype(jnp.bfloat16).reshape(group_rows, head_count, HEAD_DIM)
        val_vecs = (projected[:, 2] + qv_bias[1]).astype(jnp.bfloat16).reshape(group_rows, head_count, HEAD_DIM)
        scores = jnp.einsum('qhd,khd->hqk', queries.astype(jnp.float32), key_vecs.astype(jnp.float32)) * score_scale
        scores = jnp.where(allowed[None], scores, -jnp.inf)
        row_max = lax.optimization_barrier(jnp.max(scores, axis=-1, keepdims=True))
        log_total = row_max + jnp.log(lax.optimization_barrier(jnp.sum(jnp.exp(scores - row_max), axis=-1, keepdims=True)))
        soft_probs = jnp.exp(scores - log_total)
        probs_half = soft_probs.astype(jnp.bfloat16)
        attended = jnp.einsum('hqk,khd->qhd', probs_half.astype(jnp.float32), val_vecs.astype(jnp.float32))
        attended = attended.astype(jnp.bfloat16).reshape(group_rows, width)
        residual_mid = hidden_in + jnp.dot(attended, w_o[layer_index], preferred_element_type=jnp.float32) + bias_rows[2]
        normed_two, unit_two, inv_two = layer_norm(residual_mid, gain_rows[1], bias_rows[1])
        normed_two = normed_two.astype(jnp.bfloat16)
        pre_act = jnp.dot(normed_two, w_1[layer_index], preferred_element_type=jnp.float32) + b_ffn[layer_index].astype(jnp.float32)
        gelu_value, gelu_slope = gelu_pair(pre_act)
        activated = gelu_value.astype(jnp.bfloat16)
        hidden_out = residual_mid + jnp.dot(activated, w_2[layer_index], preferred_element_type=jnp.float32) + bias_rows[3]
        caches.append((unit_one, inv_one, normed_one, queries, key_vecs, val_vecs, soft_probs, probs_half, attended, unit_two, inv_two, normed_two, activated, gelu_slope))
        hidden_in = hidden_out
    output_rows = hidden_in
    back = grad_group
    layer_grads = [None] * LAYERS
    for layer_index in reversed(range(LAYERS)):
        unit_one, inv_one, normed_one, queries, key_vecs, val_vecs, soft_probs, probs_half, attended, unit_two, inv_two, normed_two, activated, gelu_slope = caches[layer_index]
        gain_rows = norm_gains[layer_index].astype(jnp.float32)
        grad_half = back.astype(jnp.bfloat16)
        grad_w2 = jnp.dot(activated.T, grad_half, preferred_element_type=jnp.float32)
        grad_pre = jnp.dot(grad_half, w_2[layer_index].T, preferred_element_type=jnp.float32) * gelu_slope
        grad_pre_half = grad_pre.astype(jnp.bfloat16)
        grad_w1 = jnp.dot(normed_two.T, grad_pre_half, preferred_element_type=jnp.float32)
        grad_normed_two = jnp.dot(grad_pre_half, w_1[layer_index].T, preferred_element_type=jnp.float32)
        grad_mid = back + norm_back(grad_normed_two, unit_two, inv_two, gain_rows[1])
        grad_mid_half = grad_mid.astype(jnp.bfloat16)
        grad_wo = jnp.dot(attended.T, grad_mid_half, preferred_element_type=jnp.float32)
        grad_attended = jnp.dot(grad_mid_half, w_o[layer_index].T, preferred_element_type=jnp.float32)
        grad_attended = grad_attended.astype(jnp.bfloat16).reshape(group_rows, head_count, HEAD_DIM)
        grad_probs = jnp.einsum('qhd,khd->hqk', grad_attended.astype(jnp.float32), val_vecs.astype(jnp.float32))
        row_dot = lax.optimization_barrier(jnp.sum(grad_probs * soft_probs, axis=-1, keepdims=True))
        score_grad = (soft_probs * (grad_probs - row_dot) * score_scale).astype(jnp.bfloat16)
        query_grad = jnp.einsum('hqk,khd->qhd', score_grad.astype(jnp.float32), key_vecs.astype(jnp.float32))
        key_grad = jnp.einsum('hqk,qhd->khd', score_grad.astype(jnp.float32), queries.astype(jnp.float32))
        val_grad = jnp.einsum('hqk,qhd->khd', probs_half.astype(jnp.float32), grad_attended.astype(jnp.float32))
        grad_qkv = jnp.stack([query_grad, key_grad, val_grad], axis=1).astype(jnp.bfloat16).reshape(group_rows, 3 * width)
        grad_bqv = jnp.stack([lax.optimization_barrier(jnp.sum(query_grad, axis=0)).reshape(width), lax.optimization_barrier(jnp.sum(val_grad, axis=0)).reshape(width)])
        qkv_matrix = w_qkv[layer_index].reshape(width, 3 * width)
        grad_wqkv = jnp.dot(normed_one.T, grad_qkv, preferred_element_type=jnp.float32).reshape(width, 3, width)
        grad_normed_one = jnp.dot(grad_qkv, qkv_matrix.T, preferred_element_type=jnp.float32)
        next_back = grad_mid + norm_back(grad_normed_one, unit_one, inv_one, gain_rows[0])
        grad_gains = jnp.stack([lax.optimization_barrier(jnp.sum(grad_normed_one * unit_one, axis=0)), lax.optimization_barrier(jnp.sum(grad_normed_two * unit_two, axis=0))])
        grad_vbias = jnp.stack([lax.optimization_barrier(jnp.sum(grad_normed_one, axis=0)), lax.optimization_barrier(jnp.sum(grad_normed_two, axis=0)), lax.optimization_barrier(jnp.sum(grad_mid, axis=0)), lax.optimization_barrier(jnp.sum(back, axis=0))])
        layer_grads[layer_index] = (grad_wqkv, grad_bqv, grad_wo, grad_w1, lax.optimization_barrier(jnp.sum(grad_pre, axis=0)), grad_w2, grad_gains, grad_vbias)
        back = next_back
    stacked = tuple((jnp.stack([layer_grads[index][member] for index in range(LAYERS)]) for member in range(8)))
    return (output_rows, back, stacked)

def reference(x_in, d_out, seq_lengths, w_qkv, b_qv, w_o, w_1, b_ffn, w_2, norm_gains, vec_biases):
    params = (w_qkv, b_qv, w_o, w_1, b_ffn, w_2, norm_gains, vec_biases)
    x_groups = x_in.reshape(-1, TOK_DEV, D)
    grad_groups = d_out.reshape(-1, TOK_DEV, D)
    zero_grads = tuple((jnp.zeros(weight.shape, jnp.float32) for weight in params))

    def group_step(totals, items):
        x_group, grad_group, lengths = items
        output_rows, grad_rows, grads = group_pass(x_group, grad_group, lengths, params)
        return (tuple((total + grad for total, grad in zip(totals, grads))), (output_rows, grad_rows))
    totals, (outputs, grads_x) = lax.scan(group_step, zero_grads, (x_groups, grad_groups, seq_lengths))
    return (outputs.reshape(-1, D), grads_x.reshape(-1, D), totals[0], totals[1], totals[2], totals[3], totals[4], totals[5], totals[6], totals[7])
```

```python
import math

import jax
import jax.numpy as jnp
from jax import lax
from jax.experimental import pallas as pl
from jax.experimental.pallas import tpu as pltpu
from jax.sharding import PartitionSpec as P

HEAD_DIM = 64


NORM_EPS = 1e-05
GELU_COEFF = 0.7978845608028654
GELU_CUBIC = 0.044715


def layer_norm(inputs, gain_row, bias_row):
    row_mean = jnp.mean(inputs, axis=-1, keepdims=True)
    centered = inputs - row_mean
    inv_std = lax.rsqrt(jnp.mean(centered * centered, axis=-1, keepdims=True) + NORM_EPS)
    normed = centered * inv_std
    return (normed * gain_row + bias_row, normed, inv_std)


def norm_back(grad_in, normed, inv_std, gain_row):
    scaled = grad_in * gain_row
    return inv_std * (
        scaled
        - jnp.mean(scaled, axis=-1, keepdims=True)
        - normed * jnp.mean(scaled * normed, axis=-1, keepdims=True)
    )


def gelu_pair(pre_act):
    squared = pre_act * pre_act
    tangent = jnp.tanh(GELU_COEFF * (pre_act + GELU_CUBIC * squared * pre_act))
    gelu_value = 0.5 * pre_act * (1.0 + tangent)
    gelu_slope = 0.5 * (1.0 + tangent) + 0.5 * pre_act * (1.0 - tangent * tangent) * GELU_COEFF * (
        1.0 + 3.0 * GELU_CUBIC * squared
    )
    return (gelu_value, gelu_slope)


def segment_ids(lengths, total_rows):
    sequence_ends = jnp.cumsum(lengths)
    positions = jnp.arange(total_rows, dtype=jnp.int32)
    return jnp.sum(
        (positions[:, None] >= sequence_ends[None, :]).astype(jnp.int32), axis=1, dtype=jnp.int32
    )


def contract_first(left, right):
    return lax.dot_general(
        left, right, (((0,), (0,)), ((), ())), preferred_element_type=jnp.float32
    )


def contract_last(left, right):
    return lax.dot_general(
        left, right, (((1,), (1,)), ((), ())), preferred_element_type=jnp.float32
    )

def exchange_kernel(plan, *refs):
    count = len(plan)
    ins = refs[:count]
    outs = refs[count : 2 * count]
    send_sem, recv_sem, own_sem = refs[2 * count :]

    greeted = []
    for axis in sorted({axis for axis, _, _ in plan}):
        kinds = {kind for name, kind, _ in plan if name == axis}
        size = [n for name, _, n in plan if name == axis][0]
        me = lax.axis_index(axis)
        if kinds == {"paired"}:
            greeted.append({axis: me + 1 - 2 * (me % 2)})
            greeted += [{axis: (me + k) % size} for k in range(2, size, 2)]
        else:
            greeted += [{axis: (me + k) % size} for k in range(1, size)]
    barrier = pltpu.get_barrier_semaphore()
    for device in greeted:
        pl.semaphore_signal(
            barrier, inc=1, device_id=device, device_id_type=pl.DeviceIdType.MESH
        )
    pl.semaphore_wait(barrier, len(greeted))

    used = [0]

    def remote(src, dst, device):
        slot = used[0]
        used[0] += 1
        copy = pltpu.make_async_remote_copy(
            src_ref=src,
            dst_ref=dst,
            send_sem=send_sem.at[slot],
            recv_sem=recv_sem.at[slot],
            device_id=device,
            device_id_type=pl.DeviceIdType.MESH,
        )
        copy.start()
        return copy

    started = []
    relays = []
    own = []
    for index, (axis, kind, size) in enumerate(plan):
        me = lax.axis_index(axis)
        src, dst = ins[index], outs[index]
        if kind == "paired":
            for k in range(2, size, 2):
                copy = remote(src, dst.at[me], {axis: (me + k) % size})
                relays.append((copy, dst, axis, (me + size - k) % size))
            started.append(remote(src, dst.at[me], {axis: me + 1 - 2 * (me % 2)}))
        else:
            for k in range(1, size):
                peer = (me + k) % size
                block = src if kind == "gather" else src.at[peer]
                started.append(remote(block, dst.at[me], {axis: peer}))
    for index, (axis, kind, size) in enumerate(plan):
        me = lax.axis_index(axis)
        block = ins[index].at[me] if kind == "swap" else ins[index]
        copy = pltpu.make_async_copy(block, outs[index].at[me], own_sem.at[index])
        copy.start()
        own.append(copy)
    for copy, dst, axis, slot in relays:
        copy.wait_recv()
        me = lax.axis_index(axis)
        started.append(
            remote(dst.at[slot], dst.at[slot], {axis: me + 1 - 2 * (me % 2)})
        )
    for copy, _, _, _ in relays:
        copy.wait_send()
    for copy in own:
        copy.wait()
    for copy in started:
        copy.wait()


def make_exchange():
    calls = [0]

    def exchange(*items):
        plan = []
        shapes = []
        copies = 0
        sent = 0
        for axis, kind, value in items:
            size = lax.axis_size(axis)
            if kind == "paired" and size % 2:
                kind = "gather"
            plan.append((axis, kind, size))
            copies += size - 1
            block = value.shape[1:] if kind == "swap" else value.shape
            shapes.append(jax.ShapeDtypeStruct((size,) + block, value.dtype))
            sent += (size - 1) * math.prod(block) * value.dtype.itemsize
        collective_id = calls[0]
        calls[0] += 1
        return pl.pallas_call(
            lambda *refs: exchange_kernel(tuple(plan), *refs),
            out_shape=tuple(shapes),
            in_specs=[pl.BlockSpec(memory_space=pltpu.VMEM)] * len(plan),
            out_specs=tuple([pl.BlockSpec(memory_space=pltpu.VMEM)] * len(plan)),
            scratch_shapes=[
                pltpu.SemaphoreType.DMA((copies,)),
                pltpu.SemaphoreType.DMA((copies,)),
                pltpu.SemaphoreType.DMA((len(plan),)),
            ],
            compiler_params=pltpu.CompilerParams(
                collective_id=collective_id,
                has_side_effects=True,
                vmem_limit_bytes=48 * 1024 * 1024,
            ),
            cost_estimate=pl.CostEstimate(flops=0, bytes_accessed=sent, transcendentals=0),
            name=f"exchange_{collective_id}",
        )(*[value for _, _, value in items])

    return exchange


def masked_scores(queries, key_vecs, segments, score_scale):
    positions = jnp.arange(key_vecs.shape[0], dtype=jnp.int32)
    allowed = (segments[:, None] == segments[None, :]) & (
        positions[None, :] <= positions[:, None]
    )
    scores = (
        jnp.einsum("qhd,khd->hqk", queries, key_vecs, preferred_element_type=jnp.float32)
        * score_scale
    )
    return jnp.where(allowed[None], scores, -jnp.inf)


def attend(queries, key_vecs, val_vecs, segments, score_scale):
    scores = masked_scores(queries, key_vecs, segments, score_scale)
    row_max = jnp.max(scores, axis=-1, keepdims=True)
    log_total = row_max + jnp.log(jnp.sum(jnp.exp(scores - row_max), axis=-1, keepdims=True))
    probs_half = jnp.exp(scores - log_total).astype(jnp.bfloat16)
    attended = jnp.einsum("hqk,khd->qhd", probs_half, val_vecs, preferred_element_type=jnp.float32)
    return (attended.astype(jnp.bfloat16).reshape(queries.shape[0], -1), log_total)


def attend_back(queries, key_vecs, val_vecs, grad_attended, log_total, segments, score_scale):
    scores = masked_scores(queries, key_vecs, segments, score_scale)
    soft_probs = jnp.exp(scores - log_total)
    probs_half = soft_probs.astype(jnp.bfloat16)
    grad_probs = jnp.einsum(
        "qhd,khd->hqk", grad_attended, val_vecs, preferred_element_type=jnp.float32
    )
    val_grad = jnp.einsum(
        "hqk,qhd->khd", probs_half, grad_attended, preferred_element_type=jnp.float32
    )
    row_dot = jnp.sum(grad_probs * soft_probs, axis=-1, keepdims=True)
    score_grad = (soft_probs * (grad_probs - row_dot) * score_scale).astype(jnp.bfloat16)
    query_grad = jnp.einsum(
        "hqk,khd->qhd", score_grad, key_vecs, preferred_element_type=jnp.float32
    )
    key_grad = jnp.einsum("hqk,qhd->khd", score_grad, queries, preferred_element_type=jnp.float32)
    return (query_grad, key_grad, val_grad)


def pack(pieces, width, tile):
    flat = jnp.concatenate([piece.reshape(-1) for piece in pieces])
    unit = width * tile
    return jnp.pad(flat, (0, -flat.shape[0] % unit)).reshape(-1, width)


def unpack(packed, shapes):
    flat = packed.reshape(packed.shape[0], -1)
    pieces = []
    at = 0
    for shape in shapes:
        length = math.prod(shape)
        pieces.append(flat[:, at : at + length].reshape((packed.shape[0],) + shape))
        at += length
    return pieces


def shards(x_in, d_out, seq_lengths, w_qkv, b_qv, w_o, w_1, b_ffn, w_2, norm_gains, vec_biases):
    exchange = make_exchange()
    own_rows, width = x_in.shape
    tensor_size = lax.axis_size("tensor")
    dp_size = lax.axis_size("dp")
    group_rows = own_rows * tensor_size
    layer_count = w_qkv.shape[0]
    local_width = w_qkv.shape[3]
    local_heads = local_width // HEAD_DIM
    qkv_width = 3 * local_width
    score_scale = 1.0 / math.sqrt(HEAD_DIM)
    segments = segment_ids(seq_lengths[0], group_rows)
    half = jnp.bfloat16

    def shard_of(name, layer_index):
        if name == "qkv":
            return w_qkv[layer_index].reshape(w_qkv.shape[1], qkv_width)
        if name == "out":
            return w_o[layer_index].T
        if name == "up":
            return w_1[layer_index]
        return w_2[layer_index].T

    weights = {}

    def step(tensor_items, fetched=(), sums=()):
        items = [("tensor", kind, value) for kind, value in tensor_items]
        items += [("dp", "paired", shard_of(*key)) for key in fetched]
        items += [("dp", "swap", value) for value in sums]
        results = list(exchange(*items))
        for position, key in enumerate(fetched):
            piece = results[len(tensor_items) + position]
            weights[key] = piece.reshape(dp_size * piece.shape[1], piece.shape[2])
        gathered = [
            piece.reshape(group_rows, width) if kind == "gather" else piece.astype(jnp.float32).sum(0)
            for (kind, _), piece in zip(tensor_items, results)
        ]
        totals = [
            piece.astype(jnp.float32).sum(0) for piece in results[len(items) - len(sums) :]
        ]
        return gathered, totals

    def to_owners(partial):
        return ("swap", partial.astype(half).reshape(tensor_size, own_rows, width))

    def by_owner(gradient):
        return gradient.astype(half).reshape(dp_size, -1, gradient.shape[-1])

    small_shapes = [b_qv.shape, b_ffn.shape, norm_gains.shape, vec_biases.shape]
    small = pack([b_qv, b_ffn, norm_gains, vec_biases], 128, 16)
    first = exchange(
        ("tensor", "gather", d_out.astype(half)),
        ("dp", "paired", small),
        ("dp", "paired", shard_of("qkv", 0)),
    )
    last_grad_half = first[0].reshape(group_rows, width)
    weights["qkv", 0] = first[2].reshape(width, qkv_width)
    qv_all, ffn_all, gain_all, bias_all = [
        jnp.moveaxis(piece, 0, -2).reshape(piece.shape[1:-1] + (-1,)).astype(jnp.float32)
        for piece in unpack(first[1], small_shapes)
    ]

    caches = []
    hidden_in = x_in
    for layer_index in range(layer_count):
        last = layer_index == layer_count - 1
        following = layer_index + 1
        gain_rows = gain_all[layer_index]
        bias_rows = bias_all[layer_index]
        normed_own, unit_one, inv_one = layer_norm(hidden_in, gain_rows[0], bias_rows[0])
        fetched = [("out", 0), ("up", 0)] if layer_index == 0 else [("down", layer_index)]
        (normed_one,), _ = step([("gather", normed_own.astype(half))], fetched)
        projected = jnp.dot(
            normed_one, weights["qkv", layer_index], preferred_element_type=jnp.float32
        ).reshape(group_rows, 3, local_width)
        qv_bias = qv_all[layer_index]
        heads = (group_rows, local_heads, HEAD_DIM)
        queries = (projected[:, 0] + qv_bias[0]).astype(half).reshape(heads)
        key_vecs = projected[:, 1].astype(half).reshape(heads)
        val_vecs = (projected[:, 2] + qv_bias[1]).astype(half).reshape(heads)
        attended, log_total = attend(queries, key_vecs, val_vecs, segments, score_scale)
        fetched = [("down", 0)] if layer_index == 0 else []
        (summed,), _ = step(
            [to_owners(contract_last(attended, weights["out", layer_index]))], fetched
        )
        residual_mid = hidden_in + summed + bias_rows[2]
        normed_own_two, unit_two, inv_two = layer_norm(residual_mid, gain_rows[1], bias_rows[1])
        fetched = [] if last else [("qkv", following), ("out", following)]
        (normed_two,), _ = step([("gather", normed_own_two.astype(half))], fetched)
        pre_act = (
            jnp.dot(normed_two, weights["up", layer_index], preferred_element_type=jnp.float32)
            + ffn_all[layer_index]
        )
        gelu_value, gelu_slope = gelu_pair(pre_act)
        activated = gelu_value.astype(half)
        ffn_partial = to_owners(contract_last(activated, weights["down", layer_index]))
        if not last:
            (summed,), _ = step([ffn_partial], [("up", following)])
            hidden_in = residual_mid + summed + bias_rows[3]
        caches.append(
            (
                unit_one,
                inv_one,
                normed_one,
                queries,
                key_vecs,
                val_vecs,
                attended,
                log_total,
                unit_two,
                inv_two,
                normed_two,
                activated,
                gelu_slope,
            )
        )
    back = d_out
    grads = {}
    small_terms = [None] * layer_count
    output = None
    for layer_index in reversed(range(layer_count)):
        last = layer_index == layer_count - 1
        gain_rows = gain_all[layer_index]
        (
            unit_one,
            inv_one,
            normed_one,
            queries,
            key_vecs,
            val_vecs,
            attended,
            log_total,
            unit_two,
            inv_two,
            normed_two,
            activated,
            gelu_slope,
        ) = caches[layer_index]
        if last:
            grad_half = last_grad_half
        else:
            (grad_half,), _ = step([("gather", back.astype(half))])
        grad_down = by_owner(contract_first(grad_half, activated))
        grad_pre = (
            jnp.dot(grad_half, weights["down", layer_index], preferred_element_type=jnp.float32)
            * gelu_slope
        )
        grad_pre_half = grad_pre.astype(half)
        grad_up = by_owner(contract_first(normed_two, grad_pre_half))
        partial = to_owners(contract_last(grad_pre_half, weights["up", layer_index]))
        if last:
            (grad_normed_two, summed), (grads["down", layer_index],) = step(
                [partial, ffn_partial], sums=[grad_down]
            )
            output = residual_mid + summed + bias_all[layer_index][3]
        else:
            (grad_normed_two,), (grads["down", layer_index],) = step([partial], sums=[grad_down])
        grad_mid = back + norm_back(grad_normed_two, unit_two, inv_two, gain_rows[1])
        (grad_mid_half,), (grads["up", layer_index],) = step(
            [("gather", grad_mid.astype(half))], sums=[grad_up]
        )
        grad_out = by_owner(contract_first(grad_mid_half, attended))
        grad_attended = jnp.dot(
            grad_mid_half, weights["out", layer_index], preferred_element_type=jnp.float32
        )
        grad_attended = grad_attended.astype(half).reshape(group_rows, local_heads, HEAD_DIM)
        query_grad, key_grad, val_grad = attend_back(
            queries, key_vecs, val_vecs, grad_attended, log_total, segments, score_scale
        )
        flat = (group_rows, local_width)
        grad_qkv = jnp.concatenate(
            [part.astype(half).reshape(flat) for part in (query_grad, key_grad, val_grad)], axis=1
        )
        grad_qkv_weight = by_owner(contract_first(normed_one, grad_qkv))
        (grad_normed_one,), (grads["qkv", layer_index], grads["out", layer_index]) = step(
            [to_owners(contract_last(grad_qkv, weights["qkv", layer_index]))],
            sums=[grad_qkv_weight, grad_out],
        )
        small_terms[layer_index] = (
            jnp.stack(
                [
                    jnp.sum(query_grad, axis=0).reshape(local_width),
                    jnp.sum(val_grad, axis=0).reshape(local_width),
                ]
            ),
            jnp.sum(grad_pre, axis=0),
            jnp.stack(
                [
                    jnp.sum(grad_normed_one * unit_one, axis=0),
                    jnp.sum(grad_normed_two * unit_two, axis=0),
                ]
            ),
            jnp.stack(
                [
                    jnp.sum(grad_normed_one, axis=0),
                    jnp.sum(grad_normed_two, axis=0),
                    jnp.sum(grad_mid, axis=0),
                    jnp.sum(back, axis=0),
                ]
            ),
        )
        back = grad_mid + norm_back(grad_normed_one, unit_one, inv_one, gain_rows[0])

    def split_owner(piece):
        return jnp.moveaxis(
            piece.reshape(piece.shape[:-1] + (dp_size, -1)), -2, 0
        ).reshape(dp_size, -1)

    stacked = [
        split_owner(jnp.stack([small_terms[index][member] for index in range(layer_count)]))
        for member in (2, 3, 0, 1)
    ]
    flat = jnp.concatenate(stacked, axis=1)
    flat = jnp.pad(flat, ((0, 0), (0, -flat.shape[1] % 1024)))
    (parts,) = exchange(("dp", "swap", flat.reshape(dp_size, -1, 128)))
    total = parts.sum(0)
    (shared,) = exchange(("tensor", "gather", total))
    everyone = shared.sum(0).reshape(-1)
    gain_size, bias_size = norm_gains.size, vec_biases.size
    mine = total.reshape(-1)[gain_size + bias_size :]

    def stack_layers(name, shape, transposed):
        parts = [grads[name, index] for index in range(layer_count)]
        return jnp.stack([part.T if transposed else part for part in parts]).reshape(shape)

    return (
        output,
        back,
        stack_layers("qkv", w_qkv.shape, False),
        mine[: b_qv.size].reshape(b_qv.shape),
        stack_layers("out", w_o.shape, True),
        stack_layers("up", w_1.shape, False),
        mine[b_qv.size : b_qv.size + b_ffn.size].reshape(b_ffn.shape),
        stack_layers("down", w_2.shape, True),
        everyone[:gain_size].reshape(norm_gains.shape),
        everyone[gain_size : gain_size + bias_size].reshape(vec_biases.shape),
    )


def solution(mesh):
    in_specs = (
        P(("dp", "tensor"), None),
        P(("dp", "tensor"), None),
        P("dp", None),
        P(None, "dp", None, "tensor"),
        P(None, None, ("tensor", "dp")),
        P(None, "tensor", "dp"),
        P(None, "dp", "tensor"),
        P(None, ("tensor", "dp")),
        P(None, "tensor", "dp"),
        P(None, None, "dp"),
        P(None, None, "dp"),
    )
    out_specs = (
        P(("dp", "tensor"), None),
        P(("dp", "tensor"), None),
        P(None, "dp", None, "tensor"),
        P(None, None, ("tensor", "dp")),
        P(None, "tensor", "dp"),
        P(None, "dp", "tensor"),
        P(None, ("tensor", "dp")),
        P(None, "tensor", "dp"),
        P(None, None, "dp"),
        P(None, None, "dp"),
    )
    return jax.shard_map(shards, mesh=mesh, in_specs=in_specs, out_specs=out_specs, check_vma=False)
```

```python
import math

import jax
import jax.numpy as jnp
from jax import lax
from jax.experimental import pallas as pl
from jax.experimental.pallas import tpu as pltpu
from jax.sharding import PartitionSpec as P

HEAD_DIM = 64


NORM_EPS = 1e-05
GELU_COEFF = 0.7978845608028654
GELU_CUBIC = 0.044715


def layer_norm(inputs, gain_row, bias_row):
    row_mean = jnp.mean(inputs, axis=-1, keepdims=True)
    centered = inputs - row_mean
    inv_std = lax.rsqrt(jnp.mean(centered * centered, axis=-1, keepdims=True) + NORM_EPS)
    normed = centered * inv_std
    return (normed * gain_row + bias_row, normed, inv_std)


def norm_back(grad_in, normed, inv_std, gain_row):
    scaled = grad_in * gain_row
    return inv_std * (
        scaled
        - jnp.mean(scaled, axis=-1, keepdims=True)
        - normed * jnp.mean(scaled * normed, axis=-1, keepdims=True)
    )


def gelu_pair(pre_act):
    squared = pre_act * pre_act
    tangent = jnp.tanh(GELU_COEFF * (pre_act + GELU_CUBIC * squared * pre_act))
    gelu_value = 0.5 * pre_act * (1.0 + tangent)
    gelu_slope = 0.5 * (1.0 + tangent) + 0.5 * pre_act * (1.0 - tangent * tangent) * GELU_COEFF * (
        1.0 + 3.0 * GELU_CUBIC * squared
    )
    return (gelu_value, gelu_slope)


def segment_ids(lengths, total_rows):
    sequence_ends = jnp.cumsum(lengths)
    positions = jnp.arange(total_rows, dtype=jnp.int32)
    return jnp.sum(
        (positions[:, None] >= sequence_ends[None, :]).astype(jnp.int32), axis=1, dtype=jnp.int32
    )


def contract_first(left, right):
    return lax.dot_general(
        left, right, (((0,), (0,)), ((), ())), preferred_element_type=jnp.float32
    )


def contract_last(left, right):
    return lax.dot_general(
        left, right, (((1,), (1,)), ((), ())), preferred_element_type=jnp.float32
    )

def exchange_kernel(plan, *refs):
    count = len(plan)
    ins = refs[:count]
    outs = refs[count : 2 * count]
    send_sem, recv_sem, own_sem = refs[2 * count : 2 * count + 3]
    spare = list(refs[2 * count + 3 :])

    greeted = []
    for axis in sorted({axis for axis, _, _ in plan}):
        kinds = {kind for name, kind, _ in plan if name == axis}
        size = [n for name, _, n in plan if name == axis][0]
        me = lax.axis_index(axis)
        if kinds == {"paired"}:
            greeted.append({axis: me + 1 - 2 * (me % 2)})
            greeted += [{axis: (me + k) % size} for k in range(2, size, 2)]
        else:
            greeted += [{axis: (me + k) % size} for k in range(1, size)]
    barrier = pltpu.get_barrier_semaphore()
    for device in greeted:
        pl.semaphore_signal(
            barrier, inc=1, device_id=device, device_id_type=pl.DeviceIdType.MESH
        )
    pl.semaphore_wait(barrier, len(greeted))

    used = [0]

    def remote(src, dst, device):
        slot = used[0]
        used[0] += 1
        copy = pltpu.make_async_remote_copy(
            src_ref=src,
            dst_ref=dst,
            send_sem=send_sem.at[slot],
            recv_sem=recv_sem.at[slot],
            device_id=device,
            device_id_type=pl.DeviceIdType.MESH,
        )
        copy.start()
        return copy

    def in_line(axis, src, dst, base, place, target, arrival):
        return pltpu.make_async_remote_copy(
            src_ref=src,
            dst_ref=dst,
            send_sem=send_sem.at[base + place],
            recv_sem=recv_sem.at[base + arrival],
            device_id={axis: jnp.int32(target)},
            device_id_type=pl.DeviceIdType.MESH,
        )

    def line_start(axis, kind, src, dst, base, held):
        me = lax.axis_index(axis)
        for m in range(4):

            @pl.when(me == m)
            def _(m=m):
                if kind == "sum" and m in (0, 3):
                    far = 3 - m
                    near = 1 if m == 0 else 2
                    in_line(axis, src.at[far], held, base, far, near, 4).start()
                for target in ((2, 1), (3, 2, 0), (0, 1, 3), (1, 2))[m]:
                    if kind == "sum" and (m, target) in ((1, 3), (2, 0)):
                        continue
                    block = src.at[target] if kind == "sum" else src
                    in_line(axis, block, dst.at[m], base, target, target, m).start()

    def line_relay(axis, kind, src, dst, base, held, mixed):
        me = lax.axis_index(axis)
        for m in (1, 2):

            @pl.when(me == m)
            def _(m=m):
                far = 3 if m == 1 else 0
                near = 3 - far
                if kind == "line":
                    in_line(axis, src, dst.at[far], base, far, far, far).wait_recv()
                    in_line(axis, dst.at[far], dst.at[far], base, 4, near, far).start()
                else:
                    in_line(axis, held, held, base, far, far, 4).wait_recv()

                    def add(row, carry):
                        rows = pl.ds(row * 16, 16)
                        mixed[rows] = (
                            held[rows].astype(jnp.float32)
                            + src[far, rows].astype(jnp.float32)
                        ).astype(mixed.dtype)
                        return carry

                    lax.fori_loop(0, mixed.shape[0] // 16, add, 0)
                    in_line(axis, mixed, dst.at[m], base, far, far, m).start()

        if kind == "sum":
            for m in (0, 3):

                @pl.when(me == m)
                def _(m=m):
                    dst[3 - m] = jnp.zeros(dst.shape[1:], dst.dtype)

    def line_finish(axis, kind, src, dst, base, held, mixed):
        me = lax.axis_index(axis)
        for m in range(4):

            @pl.when(me == m)
            def _(m=m):
                block = src.at[0] if kind == "sum" else src
                for other in range(4):
                    if other == m:
                        continue
                    ends = (m, other) in ((0, 3), (3, 0))
                    relayed = (m, other) in ((1, 3), (2, 0))
                    copy = in_line(axis, block, dst.at[other], base, other, other, other)
                    if not (kind == "sum" and ends) and not (kind == "line" and relayed):
                        copy.wait_recv()
                    if not (kind == "line" and ends):
                        copy.wait_send()
                if kind == "line" and m in (1, 2):
                    in_line(axis, block, dst.at[0], base, 4, 0, 0).wait_send()

    started = []
    relays = []
    own = []
    lines = []
    for index, (axis, kind, size) in enumerate(plan):
        me = lax.axis_index(axis)
        src, dst = ins[index], outs[index]
        if kind in ("line", "sum"):
            held = spare.pop(0) if kind == "sum" else None
            mixed = spare.pop(0) if kind == "sum" else None
            line_start(axis, kind, src, dst, used[0], held)
            lines.append((axis, kind, src, dst, used[0], held, mixed))
            used[0] += 5
        elif kind == "paired":
            for k in range(2, size, 2):
                copy = remote(src, dst.at[me], {axis: (me + k) % size})
                relays.append((copy, dst, axis, (me + size - k) % size))
            started.append(remote(src, dst.at[me], {axis: me + 1 - 2 * (me % 2)}))
        else:
            for k in range(1, size):
                peer = (me + k) % size
                block = src if kind == "gather" else src.at[peer]
                started.append(remote(block, dst.at[me], {axis: peer}))
    for index, (axis, kind, size) in enumerate(plan):
        me = lax.axis_index(axis)
        block = ins[index].at[me] if kind in ("swap", "sum") else ins[index]
        copy = pltpu.make_async_copy(block, outs[index].at[me], own_sem.at[index])
        copy.start()
        own.append(copy)
    for line in lines:
        line_relay(*line)
    for copy, dst, axis, slot in relays:
        copy.wait_recv()
        me = lax.axis_index(axis)
        started.append(
            remote(dst.at[slot], dst.at[slot], {axis: me + 1 - 2 * (me % 2)})
        )
    for copy, _, _, _ in relays:
        copy.wait_send()
    for copy in own:
        copy.wait()
    for copy in started:
        copy.wait()
    for line in lines:
        line_finish(*line)


def make_exchange():
    calls = [0]

    def exchange(*items):
        plan = []
        shapes = []
        copies = 0
        sent = 0
        spare = []
        for axis, kind, value in items:
            size = lax.axis_size(axis)
            if kind == "paired" and size % 2:
                kind = "gather"
            block = value.shape[1:] if kind == "swap" else value.shape
            if axis == "tensor" and size == 4 and value.dtype == jnp.bfloat16:
                kind = {"swap": "sum", "gather": "line"}[kind]
                if kind == "sum":
                    spare += [pltpu.VMEM(block, value.dtype)] * 2
            plan.append((axis, kind, size))
            copies += 5 if kind in ("line", "sum") else size - 1
            shapes.append(jax.ShapeDtypeStruct((size,) + block, value.dtype))
            sent += (size - 1) * math.prod(block) * value.dtype.itemsize
        collective_id = calls[0]
        calls[0] += 1
        return pl.pallas_call(
            lambda *refs: exchange_kernel(tuple(plan), *refs),
            out_shape=tuple(shapes),
            in_specs=[pl.BlockSpec(memory_space=pltpu.VMEM)] * len(plan),
            out_specs=tuple([pl.BlockSpec(memory_space=pltpu.VMEM)] * len(plan)),
            scratch_shapes=[
                pltpu.SemaphoreType.DMA((copies,)),
                pltpu.SemaphoreType.DMA((copies,)),
                pltpu.SemaphoreType.DMA((len(plan),)),
                *spare,
            ],
            compiler_params=pltpu.CompilerParams(
                collective_id=collective_id,
                has_side_effects=True,
                vmem_limit_bytes=48 * 1024 * 1024,
            ),
            cost_estimate=pl.CostEstimate(flops=0, bytes_accessed=sent, transcendentals=0),
            name=f"exchange_{collective_id}",
        )(*[value for _, _, value in items])

    return exchange


def masked_scores(queries, key_vecs, segments, score_scale):
    positions = jnp.arange(key_vecs.shape[0], dtype=jnp.int32)
    allowed = (segments[:, None] == segments[None, :]) & (
        positions[None, :] <= positions[:, None]
    )
    scores = (
        jnp.einsum("qhd,khd->hqk", queries, key_vecs, preferred_element_type=jnp.float32)
        * score_scale
    )
    return jnp.where(allowed[None], scores, -jnp.inf)


def attend(queries, key_vecs, val_vecs, segments, score_scale):
    scores = masked_scores(queries, key_vecs, segments, score_scale)
    row_max = jnp.max(scores, axis=-1, keepdims=True)
    log_total = row_max + jnp.log(jnp.sum(jnp.exp(scores - row_max), axis=-1, keepdims=True))
    probs_half = jnp.exp(scores - log_total).astype(jnp.bfloat16)
    attended = jnp.einsum("hqk,khd->qhd", probs_half, val_vecs, preferred_element_type=jnp.float32)
    return (attended.astype(jnp.bfloat16).reshape(queries.shape[0], -1), log_total)


def attend_back(queries, key_vecs, val_vecs, grad_attended, log_total, segments, score_scale):
    scores = masked_scores(queries, key_vecs, segments, score_scale)
    soft_probs = jnp.exp(scores - log_total)
    probs_half = soft_probs.astype(jnp.bfloat16)
    grad_probs = jnp.einsum(
        "qhd,khd->hqk", grad_attended, val_vecs, preferred_element_type=jnp.float32
    )
    val_grad = jnp.einsum(
        "hqk,qhd->khd", probs_half, grad_attended, preferred_element_type=jnp.float32
    )
    row_dot = jnp.sum(grad_probs * soft_probs, axis=-1, keepdims=True)
    score_grad = (soft_probs * (grad_probs - row_dot) * score_scale).astype(jnp.bfloat16)
    query_grad = jnp.einsum(
        "hqk,khd->qhd", score_grad, key_vecs, preferred_element_type=jnp.float32
    )
    key_grad = jnp.einsum("hqk,qhd->khd", score_grad, queries, preferred_element_type=jnp.float32)
    return (query_grad, key_grad, val_grad)


def pack(pieces, width, tile):
    flat = jnp.concatenate([piece.reshape(-1) for piece in pieces])
    unit = width * tile
    return jnp.pad(flat, (0, -flat.shape[0] % unit)).reshape(-1, width)


def unpack(packed, shapes):
    flat = packed.reshape(packed.shape[0], -1)
    pieces = []
    at = 0
    for shape in shapes:
        length = math.prod(shape)
        pieces.append(flat[:, at : at + length].reshape((packed.shape[0],) + shape))
        at += length
    return pieces


def shards(x_in, d_out, seq_lengths, w_qkv, b_qv, w_o, w_1, b_ffn, w_2, norm_gains, vec_biases):
    exchange = make_exchange()
    own_rows, width = x_in.shape
    tensor_size = lax.axis_size("tensor")
    dp_size = lax.axis_size("dp")
    group_rows = own_rows * tensor_size
    layer_count = w_qkv.shape[0]
    local_width = w_qkv.shape[3]
    local_heads = local_width // HEAD_DIM
    qkv_width = 3 * local_width
    score_scale = 1.0 / math.sqrt(HEAD_DIM)
    segments = segment_ids(seq_lengths[0], group_rows)
    half = jnp.bfloat16

    def shard_of(name, layer_index):
        if name == "qkv":
            return w_qkv[layer_index].reshape(w_qkv.shape[1], qkv_width)
        if name == "out":
            return w_o[layer_index].T
        if name == "up":
            return w_1[layer_index]
        return w_2[layer_index].T

    weights = {}

    def step(tensor_items, fetched=(), sums=()):
        items = [("tensor", kind, value) for kind, value in tensor_items]
        items += [("dp", "paired", shard_of(*key)) for key in fetched]
        items += [("dp", "swap", value) for value in sums]
        results = list(exchange(*items))
        for position, key in enumerate(fetched):
            piece = results[len(tensor_items) + position]
            weights[key] = piece.reshape(dp_size * piece.shape[1], piece.shape[2])
        gathered = [
            piece.reshape(group_rows, width) if kind == "gather" else piece.astype(jnp.float32).sum(0)
            for (kind, _), piece in zip(tensor_items, results)
        ]
        totals = [
            piece.astype(jnp.float32).sum(0) for piece in results[len(items) - len(sums) :]
        ]
        return gathered, totals

    def to_owners(partial):
        return ("swap", partial.astype(half).reshape(tensor_size, own_rows, width))

    def by_owner(gradient):
        return gradient.astype(half).reshape(dp_size, -1, gradient.shape[-1])

    small_shapes = [b_qv.shape, b_ffn.shape, norm_gains.shape, vec_biases.shape]
    small = pack([b_qv, b_ffn, norm_gains, vec_biases], 128, 16)
    first = exchange(
        ("tensor", "gather", d_out.astype(half)),
        ("dp", "paired", small),
        ("dp", "paired", shard_of("qkv", 0)),
    )
    last_grad_half = first[0].reshape(group_rows, width)
    weights["qkv", 0] = first[2].reshape(width, qkv_width)
    qv_all, ffn_all, gain_all, bias_all = [
        jnp.moveaxis(piece, 0, -2).reshape(piece.shape[1:-1] + (-1,)).astype(jnp.float32)
        for piece in unpack(first[1], small_shapes)
    ]

    caches = []
    hidden_in = x_in
    for layer_index in range(layer_count):
        last = layer_index == layer_count - 1
        following = layer_index + 1
        gain_rows = gain_all[layer_index]
        bias_rows = bias_all[layer_index]
        normed_own, unit_one, inv_one = layer_norm(hidden_in, gain_rows[0], bias_rows[0])
        fetched = [("out", 0), ("up", 0)] if layer_index == 0 else [("down", layer_index)]
        (normed_one,), _ = step([("gather", normed_own.astype(half))], fetched)
        projected = jnp.dot(
            normed_one, weights["qkv", layer_index], preferred_element_type=jnp.float32
        ).reshape(group_rows, 3, local_width)
        qv_bias = qv_all[layer_index]
        heads = (group_rows, local_heads, HEAD_DIM)
        queries = (projected[:, 0] + qv_bias[0]).astype(half).reshape(heads)
        key_vecs = projected[:, 1].astype(half).reshape(heads)
        val_vecs = (projected[:, 2] + qv_bias[1]).astype(half).reshape(heads)
        attended, log_total = attend(queries, key_vecs, val_vecs, segments, score_scale)
        fetched = [("down", 0)] if layer_index == 0 else []
        (summed,), _ = step(
            [to_owners(contract_last(attended, weights["out", layer_index]))], fetched
        )
        residual_mid = hidden_in + summed + bias_rows[2]
        normed_own_two, unit_two, inv_two = layer_norm(residual_mid, gain_rows[1], bias_rows[1])
        fetched = [] if last else [("qkv", following), ("out", following)]
        (normed_two,), _ = step([("gather", normed_own_two.astype(half))], fetched)
        pre_act = (
            jnp.dot(normed_two, weights["up", layer_index], preferred_element_type=jnp.float32)
            + ffn_all[layer_index]
        )
        gelu_value, gelu_slope = gelu_pair(pre_act)
        activated = gelu_value.astype(half)
        ffn_partial = to_owners(contract_last(activated, weights["down", layer_index]))
        if not last:
            (summed,), _ = step([ffn_partial], [("up", following)])
            hidden_in = residual_mid + summed + bias_rows[3]
        caches.append(
            (
                unit_one,
                inv_one,
                normed_one,
                queries,
                key_vecs,
                val_vecs,
                attended,
                log_total,
                unit_two,
                inv_two,
                normed_two,
                activated,
                gelu_slope,
            )
        )
    back = d_out
    grads = {}
    small_terms = [None] * layer_count
    output = None
    for layer_index in reversed(range(layer_count)):
        last = layer_index == layer_count - 1
        gain_rows = gain_all[layer_index]
        (
            unit_one,
            inv_one,
            normed_one,
            queries,
            key_vecs,
            val_vecs,
            attended,
            log_total,
            unit_two,
            inv_two,
            normed_two,
            activated,
            gelu_slope,
        ) = caches[layer_index]
        if last:
            grad_half = last_grad_half
        else:
            (grad_half,), (grads["qkv", layer_index + 1],) = step(
                [("gather", back.astype(half))], sums=[waiting]
            )
        grad_down = by_owner(contract_first(grad_half, activated))
        grad_pre = (
            jnp.dot(grad_half, weights["down", layer_index], preferred_element_type=jnp.float32)
            * gelu_slope
        )
        grad_pre_half = grad_pre.astype(half)
        grad_up = by_owner(contract_first(normed_two, grad_pre_half))
        partial = to_owners(contract_last(grad_pre_half, weights["up", layer_index]))
        if last:
            cut = grad_up.shape[2] // 2
            (grad_normed_two, summed), (grads["down", layer_index], up_left) = step(
                [partial, ffn_partial], sums=[grad_down, grad_up[:, :, :cut]]
            )
            output = residual_mid + summed + bias_all[layer_index][3]
        else:
            (grad_normed_two,), (grads["down", layer_index],) = step([partial], sums=[grad_down])
        grad_mid = back + norm_back(grad_normed_two, unit_two, inv_two, gain_rows[1])
        (grad_mid_half,), (up_part,) = step(
            [("gather", grad_mid.astype(half))], sums=[grad_up[:, :, cut:] if last else grad_up]
        )
        grads["up", layer_index] = (
            jnp.concatenate([up_left, up_part], axis=1) if last else up_part
        )
        grad_out = by_owner(contract_first(grad_mid_half, attended))
        grad_attended = jnp.dot(
            grad_mid_half, weights["out", layer_index], preferred_element_type=jnp.float32
        )
        grad_attended = grad_attended.astype(half).reshape(group_rows, local_heads, HEAD_DIM)
        query_grad, key_grad, val_grad = attend_back(
            queries, key_vecs, val_vecs, grad_attended, log_total, segments, score_scale
        )
        flat = (group_rows, local_width)
        grad_qkv = jnp.concatenate(
            [part.astype(half).reshape(flat) for part in (query_grad, key_grad, val_grad)], axis=1
        )
        grad_qkv_weight = by_owner(contract_first(normed_one, grad_qkv))
        (grad_normed_one,), sent_now = step(
            [to_owners(contract_last(grad_qkv, weights["qkv", layer_index]))],
            sums=[grad_out] if layer_index else [grad_out, grad_qkv_weight],
        )
        grads["out", layer_index] = sent_now[0]
        if layer_index:
            waiting = grad_qkv_weight
        else:
            grads["qkv", layer_index] = sent_now[1]
        small_terms[layer_index] = (
            jnp.stack(
                [
                    jnp.sum(query_grad, axis=0).reshape(local_width),
                    jnp.sum(val_grad, axis=0).reshape(local_width),
                ]
            ),
            jnp.sum(grad_pre, axis=0),
            jnp.stack(
                [
                    jnp.sum(grad_normed_one * unit_one, axis=0),
                    jnp.sum(grad_normed_two * unit_two, axis=0),
                ]
            ),
            jnp.stack(
                [
                    jnp.sum(grad_normed_one, axis=0),
                    jnp.sum(grad_normed_two, axis=0),
                    jnp.sum(grad_mid, axis=0),
                    jnp.sum(back, axis=0),
                ]
            ),
        )
        back = grad_mid + norm_back(grad_normed_one, unit_one, inv_one, gain_rows[0])

    def split_owner(piece):
        return jnp.moveaxis(
            piece.reshape(piece.shape[:-1] + (dp_size, -1)), -2, 0
        ).reshape(dp_size, -1)

    stacked = [
        split_owner(jnp.stack([small_terms[index][member] for index in range(layer_count)]))
        for member in (2, 3, 0, 1)
    ]
    flat = jnp.concatenate(stacked, axis=1)
    flat = jnp.pad(flat, ((0, 0), (0, -flat.shape[1] % 1024)))
    (parts,) = exchange(("dp", "swap", flat.reshape(dp_size, -1, 128)))
    total = parts.sum(0)
    (shared,) = exchange(("tensor", "gather", total))
    everyone = shared.sum(0).reshape(-1)
    gain_size, bias_size = norm_gains.size, vec_biases.size
    mine = total.reshape(-1)[gain_size + bias_size :]

    def stack_layers(name, shape, transposed):
        parts = [grads[name, index] for index in range(layer_count)]
        return jnp.stack([part.T if transposed else part for part in parts]).reshape(shape)

    return (
        output,
        back,
        stack_layers("qkv", w_qkv.shape, False),
        mine[: b_qv.size].reshape(b_qv.shape),
        stack_layers("out", w_o.shape, True),
        stack_layers("up", w_1.shape, False),
        mine[b_qv.size : b_qv.size + b_ffn.size].reshape(b_ffn.shape),
        stack_layers("down", w_2.shape, True),
        everyone[:gain_size].reshape(norm_gains.shape),
        everyone[gain_size : gain_size + bias_size].reshape(vec_biases.shape),
    )


def solution(mesh):
    in_specs = (
        P(("dp", "tensor"), None),
        P(("dp", "tensor"), None),
        P("dp", None),
        P(None, "dp", None, "tensor"),
        P(None, None, ("tensor", "dp")),
        P(None, "tensor", "dp"),
        P(None, "dp", "tensor"),
        P(None, ("tensor", "dp")),
        P(None, "tensor", "dp"),
        P(None, None, "dp"),
        P(None, None, "dp"),
    )
    out_specs = (
        P(("dp", "tensor"), None),
        P(("dp", "tensor"), None),
        P(None, "dp", None, "tensor"),
        P(None, None, ("tensor", "dp")),
        P(None, "tensor", "dp"),
        P(None, "dp", "tensor"),
        P(None, ("tensor", "dp")),
        P(None, "tensor", "dp"),
        P(None, None, "dp"),
        P(None, None, "dp"),
    )
    return jax.shard_map(shards, mesh=mesh, in_specs=in_specs, out_specs=out_specs, check_vma=False)
```
